128 devices in a mesh: shard: 32 (over z, x, core), tensor: 4 (over y).
Axes of the slice: x: 4, y: 4, z: 4, core: 2. Of those that a mesh axis runs over, the one named last changes fastest.
Arguments:
- attn_grads: float32 [4, 2048, 2048], P(None, 'tensor', 'shard'), may hold values from -400 to 400
- mlp_grads: float32 [3, 5120, 2048], P(None, 'tensor', 'shard'), may hold values from -400 to 400
- attn_master: float32 [4, 4194304], P(None, ('shard', 'tensor')), may hold values from -0.75 to 0.75
- attn_first: float32 [4, 4194304], P(None, ('shard', 'tensor')), may hold values from -4 to 4
- attn_second: float32 [4, 4194304], P(None, ('shard', 'tensor')), may hold values from 0.01 to 1
- attn_average: float32 [4, 4194304], P(None, ('shard', 'tensor')), may hold values from -0.75 to 0.75
- mlp_master: float32 [3, 10485760], P(None, ('shard', 'tensor')), may hold values from -0.75 to 0.75
- mlp_first: float32 [3, 10485760], P(None, ('shard', 'tensor')), may hold values from -4 to 4
- mlp_second: float32 [3, 10485760], P(None, ('shard', 'tensor')), may hold values from 0.01 to 1
- mlp_average: float32 [3, 10485760], P(None, ('shard', 'tensor')), may hold values from -0.75 to 0.75
Outputs:
- attn_master_new: float32 [4, 4194304], P(None, ('shard', 'tensor'))
- attn_first_new: float32 [4, 4194304], P(None, ('shard', 'tensor'))
- attn_second_new: float32 [4, 4194304], P(None, ('shard', 'tensor'))
- attn_average_new: float32 [4, 4194304], P(None, ('shard', 'tensor'))
- mlp_master_new: float32 [3, 10485760], P(None, ('shard', 'tensor'))
- mlp_first_new: float32 [3, 10485760], P(None, ('shard', 'tensor'))
- mlp_second_new: float32 [3, 10485760], P(None, ('shard', 'tensor'))
- mlp_average_new: float32 [3, 10485760], P(None, ('shard', 'tensor'))
- attn_weights: bfloat16 [4, 2048, 2048], P(None, 'tensor', 'shard')
- mlp_weights: bfloat16 [3, 5120, 2048], P(None, 'tensor', 'shard')
The draws below stay inside these ranges and needn't reach their ends.
All inputs are finite; a program needn't handle non-finite values.
Results may differ from the reference program's by a relative error of at most 0.0035.
Values may be sent and summed in bfloat16 or wider, within the bound.
A program may use at most 128 MiB of HBM per device.

```python
import math
import jax
import jax.numpy as jnp

D = 2048
FF = 5120
STEP = 100
HD = 2048
COUNT = 48234496


def level_factor(key, row_count, divisor):
    period = max(1, row_count // divisor)
    key_order, key_jitter = jax.random.split(key)
    order = jax.random.permutation(key_order, 4)
    base_levels = jnp.array([1.5, 0.75, 0.35, 0.15], jnp.float32)
    jitter = jnp.exp(jax.random.uniform(key_jitter, (4,), jnp.float32, math.log(0.85), math.log(1.15)))
    table = base_levels[order] * jitter
    band = jnp.arange(row_count, dtype=jnp.int32) // period % 4
    return table[band].reshape(1, row_count, 1)


def scaled_grads(key, member_count, row_count):
    key_row = jax.random.fold_in(key, 0)
    key_col = jax.random.fold_in(key, 1)
    key_base = jax.random.fold_in(key, 2)
    key_fine = jax.random.fold_in(key, 4)
    key_coarse = jax.random.fold_in(key, 5)
    row_scale = jax.random.uniform(key_row, (member_count, row_count, 1), jnp.float32, 0.8, 1.0)
    row_scale = row_scale * level_factor(key_fine, row_count, 128) * level_factor(key_coarse, row_count, 32)
    ramp = jnp.sqrt(1.0 + 2.0 * jnp.arange(D, dtype=jnp.float32) / D)
    col_scale = jnp.exp(jax.random.uniform(key_col, (1, 1, D), jnp.float32, math.log(0.3), math.log(3.0))) * ramp
    position = jnp.arange(row_count, dtype=jnp.float32).reshape(1, row_count, 1) / row_count
    row_ramp = jnp.sqrt(1.0 + 4.0 * position)
    values = jnp.clip(jax.random.normal(key_base, (member_count, row_count, D), jnp.float32), -6.0, 6.0)
    return values * row_scale * col_scale * row_ramp


def draw_attn_grads(key, part):
    return scaled_grads(jax.random.fold_in(key, 11), 4, HD)


def draw_mlp_grads(key, part):
    return scaled_grads(jax.random.fold_in(key, 12), 3, FF)


def shard_levels(stream_key, dims, cuts, low, top_value):
    level, own = 1.0, jax.random.fold_in(stream_key, 6)
    for dim, blocks in cuts:
        steps = jnp.exp(jax.random.uniform(jax.random.fold_in(own, dim), (blocks,), jnp.float32, low / len(cuts), top_value / len(cuts)))
        level = level * jnp.repeat(steps, dims[dim] // blocks).reshape([-1 if axis == dim else 1 for axis in range(len(dims))])
    return level


def gaussian(own_key, extent, scale, limit, shards=(), kind=jnp.bfloat16):
    values = jax.random.normal(own_key, extent, jnp.float32) * scale
    if len(shards) > 0:
        values = shard_levels(own_key, extent, shards, -0.22, 0.18) * values
    return jnp.clip(values, min=-limit, max=limit).astype(kind)


def setup_inputs(seed: int = 0) -> dict:
    seeds = jax.random.split(jax.random.key(seed), 11)
    return {
        "attn_grads": draw_attn_grads(jax.random.fold_in(seeds[10], 71), 0),
        "mlp_grads": draw_mlp_grads(jax.random.fold_in(seeds[10], 71), 0),
        "attn_master": gaussian(seeds[2], (4, HD * D), 0.05, 0.75, ((1, 128),), jnp.float32),
        "attn_first": gaussian(seeds[3], (4, HD * D), 0.5, 4.0, ((1, 128),), jnp.float32),
        "attn_second": jnp.clip(jnp.exp(math.log(1.0) - 4.6051702 * jax.random.uniform(seeds[4], (4, HD * D), jnp.float32) ** shard_levels(seeds[4], (4, HD * D), ((1, 128),), -0.2, 0.2)), 0.01, 1.0),
        "attn_average": gaussian(seeds[5], (4, HD * D), 0.05, 0.75, ((1, 128),), jnp.float32),
        "mlp_master": gaussian(seeds[6], (3, FF * D), 0.05, 0.75, ((1, 128),), jnp.float32),
        "mlp_first": gaussian(seeds[7], (3, FF * D), 0.5, 4.0, ((1, 128),), jnp.float32),
        "mlp_second": jnp.clip(jnp.exp(math.log(1.0) - 4.6051702 * jax.random.uniform(seeds[8], (3, FF * D), jnp.float32) ** shard_levels(seeds[8], (3, FF * D), ((1, 128),), -0.2, 0.2)), 0.01, 1.0),
        "mlp_average": gaussian(seeds[9], (3, FF * D), 0.05, 0.75, ((1, 128),), jnp.float32),
    }


beta_one = 0.9
beta_two = 0.999
adam_eps = 1e-08
learn_rate = 0.01
decay_weight = 0.1
average_keep = 0.999
clip_level = 1.0

def advance(flat_grads, master, first_moment, second, average, clip_factor):
    clipped = clip_factor * flat_grads
    first_new = beta_one * first_moment + (1.0 - beta_one) * clipped
    second_new = beta_two * second + (1.0 - beta_two) * clipped * clipped
    update = first_new / (1.0 - beta_one ** STEP) / (jnp.sqrt(second_new / (1.0 - beta_two ** STEP)) + adam_eps)
    master_new = master - learn_rate * (update + decay_weight * master)
    average_new = average_keep * average + (1.0 - average_keep) * master_new
    return (master_new, first_new, second_new, average_new)

def reference(attn_grads, mlp_grads, attn_master, attn_first, attn_second, attn_average, mlp_master, mlp_first, mlp_second, mlp_average):
    attn_flat = attn_grads.reshape(attn_grads.shape[0], -1)
    mlp_flat = mlp_grads.reshape(mlp_grads.shape[0], -1)
    grand_total = jnp.sum(attn_flat * attn_flat) + jnp.sum(mlp_flat * mlp_flat)
    clip_factor = jnp.minimum(1.0, clip_level / jnp.sqrt(grand_total / COUNT + 1e-06))
    attn_out = advance(attn_flat, attn_master, attn_first, attn_second, attn_average, clip_factor)
    mlp_out = advance(mlp_flat, mlp_master, mlp_first, mlp_second, mlp_average, clip_factor)
    attn_weights = attn_out[0].astype(jnp.bfloat16).reshape(attn_grads.shape)
    mlp_weights = mlp_out[0].astype(jnp.bfloat16).reshape(mlp_grads.shape)
    return (attn_out[0], attn_out[1], attn_out[2], attn_out[3], mlp_out[0], mlp_out[1], mlp_out[2], mlp_out[3], attn_weights, mlp_weights)
```

```python
import functools

import jax
import jax.numpy as jnp
from jax import lax
from jax.experimental import pallas as pl
from jax.experimental.pallas import tpu as pltpu
from jax.sharding import PartitionSpec as P

D = 2048
STEP = 100
COUNT = 48234496

beta_one = 0.9
beta_two = 0.999
adam_eps = 1e-08
learn_rate = 0.01
decay_weight = 0.1
average_keep = 0.999
clip_level = 1.0

MESH = pl.DeviceIdType.MESH
ROWS = 96
F32 = jnp.float32
BF16 = jnp.bfloat16


def advance(grads, master, first, second, clip):
    clipped = clip * grads
    first_new = beta_one * first + (1.0 - beta_one) * clipped
    second_new = beta_two * second + (1.0 - beta_two) * clipped * clipped
    update = (first_new * (1.0 / (1.0 - beta_one**STEP))) / (
        jnp.sqrt(second_new * (1.0 / (1.0 - beta_two**STEP))) + adam_eps
    )
    master_new = master - learn_rate * (update + decay_weight * master)
    return master_new, first_new, second_new


def low_lanes(rows):
    return lax.broadcasted_iota(jnp.int32, (rows, 128), 1) < 64


def split_halves(p_zero, p_one):
    low = low_lanes(p_zero.shape[0])
    return jnp.where(low, p_zero, p_one), pltpu.roll(jnp.where(low, p_one, p_zero), 64, 1)


def position():
    s = lax.axis_index("shard")
    return s // 8, (s // 2) % 4, s % 2, lax.axis_index("tensor")


def device(z, x, c, y):
    return (z * 8 + x * 2 + c, y)


def wait_for(ref, sem):
    pltpu.make_async_copy(ref, ref, sem).wait()


OTHERS = [(dx, dc) for dx in range(4) for dc in range(2)][1:]


class Exchange:
    def __init__(self, forward, held, landed, a_recv, b_recv, c_recv, a_sent, b_sent, c_sent):
        self.held, self.landed = held, landed
        self.a_recv, self.b_recv, self.c_recv = a_recv, b_recv, c_recv
        self.a_sent, self.b_sent, self.c_sent = a_sent, b_sent, c_sent
        self.z, self.x, self.c, self.y = position()
        self.forward = forward
        self.a, self.b = (self.y, self.z) if forward else (self.z, self.y)
        self.mine = self.x * 2 + self.c

    def at(self, a, x, c, b):
        return device(b, x, c, a) if self.forward else device(a, x, c, b)

    def send_a(self, da, xc):
        pltpu.make_async_remote_copy(
            src_ref=self.held.at[3 + da, xc],
            dst_ref=self.held.at[da, xc],
            send_sem=self.a_sent,
            recv_sem=self.a_recv.at[da, xc],
            device_id=self.at((self.a + da) % 4, self.x, self.c, self.b),
            device_id_type=MESH,
        ).start()

    def pass_b(self, da):
        origin = (self.a + 4 - da) % 4
        slot = jnp.where(origin == self.b, origin, 4 + origin)

        def take(xc):
            if da:
                wait_for(self.held.at[da, xc], self.a_recv.at[da, xc])

        for dx, dc in OTHERS:
            x, c = (self.x + dx) % 4, (self.c + dc) % 2
            xc = x * 2 + c
            take(xc)
            pltpu.make_async_remote_copy(
                src_ref=self.held.at[da, xc],
                dst_ref=self.landed.at[slot, self.mine],
                send_sem=self.b_sent.at[da],
                recv_sem=self.b_recv.at[origin, self.mine],
                device_id=self.at(self.a, x, c, self.b),
                device_id_type=MESH,
            ).start()
        take(self.mine)
        pltpu.make_async_copy(
            self.held.at[da, self.mine],
            self.landed.at[slot, self.mine],
            self.b_recv.at[origin, self.mine],
        ).start()

    def pass_c(self, da):
        origin = (self.a + 4 - da) % 4
        slot = jnp.where(origin == self.b, origin, 4 + origin)
        for xc in range(8):
            wait_for(self.landed.at[slot, xc], self.b_recv.at[origin, xc])

            @pl.when(origin != self.b)
            def _():
                pltpu.make_async_remote_copy(
                    src_ref=self.landed.at[slot, xc],
                    dst_ref=self.landed.at[self.b, xc],
                    send_sem=self.c_sent,
                    recv_sem=self.c_recv.at[self.b, xc],
                    device_id=self.at(self.a, self.x, self.c, origin),
                    device_id_type=MESH,
                ).start()

    def take_c(self, source, xc):
        wait_for(self.landed.at[source, xc], self.c_recv.at[source, xc])

    def drain(self):
        wait_for(self.held.at[pl.ds(4, 3)], self.a_sent)
        for da in range(4):
            wait_for(self.held.at[da, pl.ds(0, 7)], self.b_sent.at[da])
        wait_for(self.held.at[pl.ds(4, 3)], self.c_sent)


def exchange_kernel(
    attn_grads,
    mlp_grads,
    attn_master,
    attn_first,
    attn_second,
    mlp_master,
    mlp_first,
    mlp_second,
    attn_out,
    mlp_out,
    clip_out,
    back,
    stack_attn,
    stack_mlp,
    turned_attn,
    turned_mlp,
    held,
    landed,
    held_back,
    state_attn,
    state_mlp,
    flat_attn,
    flat_mlp,
    sums,
    grad_sem,
    state_sem,
    flat_sem,
    sum_recv,
    sum_sent,
    fa_recv,
    fb_recv,
    fc_recv,
    fa_sent,
    fb_sent,
    fc_sent,
    ra_recv,
    rb_recv,
    rc_recv,
    ra_sent,
    rb_sent,
    rc_sent,
):
    z, x, c, y = position()
    barrier = pltpu.get_barrier_semaphore()
    for d in range(1, 4):
        pl.semaphore_signal(barrier, inc=1, device_id=device(z, x, c, (y + d) % 4), device_id_type=MESH)
        pl.semaphore_signal(barrier, inc=1, device_id=device((z + d) % 4, x, c, y), device_id_type=MESH)
    for dx, dc in OTHERS:
        pl.semaphore_signal(barrier, inc=1, device_id=device(z, (x + dx) % 4, (c + dc) % 2, y), device_id_type=MESH)

    for pair in range(2):
        for i in range(2):
            half = pl.ds(pl.multiple_of(64 * ((i + c) % 2), 64), 64)
            pltpu.make_async_copy(attn_grads.at[2 * pair + i], stack_attn.at[pair, half, :], grad_sem.at[0]).start()
    for i in range(2):
        half = pl.ds(pl.multiple_of(64 * ((i + c) % 2), 64), 64)
        pltpu.make_async_copy(mlp_grads.at[i], stack_mlp.at[0, half, :], grad_sem.at[1]).start()
        pltpu.make_async_copy(mlp_grads.at[2], stack_mlp.at[1, pl.ds(64 * i, 64), :], grad_sem.at[1]).start()
    for k, (attn, mlp) in enumerate(((attn_master, mlp_master), (attn_first, mlp_first), (attn_second, mlp_second))):

        def fetch(cb, carry, k=k, attn=attn, mlp=mlp):
            for m in range(4):
                pltpu.make_async_copy(attn.at[:, cb, m, :], state_attn.at[k, cb, m], state_sem.at[0]).start()
            for m in range(3):
                pltpu.make_async_copy(mlp.at[:, cb, m, :], state_mlp.at[k, cb, m], state_sem.at[1]).start()
            return carry

        lax.fori_loop(0, 16, fetch, 0)
    turned_mlp[1, pl.ds(1280, 8), :] = jnp.zeros((8, 128), F32)

    wait_for(stack_attn, grad_sem.at[0])
    wait_for(stack_mlp, grad_sem.at[1])

    def squares(value):
        return jnp.sum((value * value).reshape(-1, 8, value.shape[-1] // 128, 128), axis=(0, 2))

    total = jnp.zeros((8, 128), F32)
    for pair in range(2):
        for b in range(4):
            block = stack_attn[pair, :, b * 128 : (b + 1) * 128]
            total = total + jnp.sum((block * block).reshape(16, 8, 128), axis=0)
            turned_attn[pair, b * 128 : (b + 1) * 128, :] = block.T
    for b in range(10):
        block = stack_mlp[0, :, b * 128 : (b + 1) * 128]
        total = total + jnp.sum((block * block).reshape(16, 8, 128), axis=0)
        turned_mlp[0, b * 128 : (b + 1) * 128, :] = block.T
        block = stack_mlp[1, :, b * 128 : (b + 1) * 128]
        turned_mlp[1, b * 128 : (b + 1) * 128, :] = block.T
        block = block[:64]
        total = total + jnp.sum((block * block).reshape(8, 8, 128), axis=0)
    sums[0] = total

    straight = (low_lanes(24).astype(jnp.int32) + c) == 1

    def pack(xc, carry):
        for dest in range(4):
            j = xc * 4 + dest
            a_rows = pl.ds(pl.multiple_of(j * 16, 16), 16)
            m_rows = pl.ds(pl.multiple_of(j * 40, 8), 40)
            t_rows = pl.ds(pl.multiple_of(j * 40, 8), 24)
            u_rows = pl.ds(pl.multiple_of(j * 40 + 24, 8), 24)
            packed = jnp.concatenate(
                [
                    turned_attn[0, a_rows, :],
                    turned_attn[1, a_rows, :],
                    turned_mlp[0, m_rows, :],
                    jnp.where(straight, turned_mlp[1, t_rows, :], turned_mlp[1, u_rows, :]),
                ],
                axis=0,
            ).astype(BF16)
            da = (dest + 4 - y) % 4
            held[jnp.where(da == 0, 0, 3 + da), xc] = packed
        return carry

    lax.fori_loop(0, 8, pack, 0)

    pl.semaphore_wait(barrier, 13)

    def send_sum(src, slot, dev):
        pltpu.make_async_remote_copy(
            src_ref=sums.at[src],
            dst_ref=sums.at[slot],
            send_sem=sum_sent.at[slot],
            recv_sem=sum_recv.at[slot],
            device_id=dev,
            device_id_type=MESH,
        ).start()

    for d in range(1, 4):
        send_sum(0, 2 + d, device(z, x, c, (y + d) % 4))

    go = Exchange(True, held, landed, fa_recv, fb_recv, fc_recv, fa_sent, fb_sent, fc_sent)
    for da in (1, 3, 2):
        for xc in range(8):
            go.send_a(da, xc)
    go.pass_b(0)

    for slot in range(3, 6):
        wait_for(sums.at[slot], sum_recv.at[slot])
    sums[1] = sums[0] + sums[3] + sums[4] + sums[5]
    for k, (dx, dc) in enumerate(OTHERS):
        send_sum(1, 6 + k, device(z, (x + dx) % 4, (c + dc) % 2, y))

    go.pass_b(1)
    go.pass_c(0)

    for slot in range(6, 13):
        wait_for(sums.at[slot], sum_recv.at[slot])
    value = sums[1]
    for slot in range(6, 13):
        value = value + sums[slot]
    sums[2] = value
    for d in range(1, 4):
        send_sum(2, 12 + d, device((z + d) % 4, x, c, y))

    go.pass_b(3)
    go.pass_c(1)
    go.pass_b(2)
    go.pass_c(3)
    go.pass_c(2)

    for slot in range(13, 16):
        wait_for(sums.at[slot], sum_recv.at[slot])
    grand = jnp.sum(sums[2] + sums[13] + sums[14] + sums[15], keepdims=True)
    clip = jnp.minimum(1.0, clip_level / jnp.sqrt(grand / COUNT + 1e-06))
    clip_out[...] = jnp.broadcast_to(clip, (8, 128))

    wait_for(state_attn, state_sem.at[0])
    wait_for(state_mlp, state_sem.at[1])

    ret = Exchange(False, held_back, back, ra_recv, rb_recv, rc_recv, ra_sent, rb_sent, rc_sent)
    low = low_lanes(ROWS)

    def work(dz):
        source = (z + dz) % 4

        def one(xs, carry):
            if dz:
                go.take_c(source, xs * 2)
                go.take_c(source, xs * 2 + 1)
            cb = source * 4 + xs
            even, odd = split_halves(landed[source, xs * 2].astype(F32), landed[source, xs * 2 + 1].astype(F32))
            grads = (
                (flat_attn, state_attn, 0, 0, 16, even[0:16]),
                (flat_attn, state_attn, 2, 0, 16, even[16:32]),
                (flat_mlp, state_mlp, 0, 0, 40, even[32:72]),
                (flat_mlp, state_mlp, 2, 0, 24, even[72:96]),
                (flat_attn, state_attn, 1, 0, 16, odd[0:16]),
                (flat_attn, state_attn, 3, 0, 16, odd[16:32]),
                (flat_mlp, state_mlp, 1, 0, 40, odd[32:72]),
                (flat_mlp, state_mlp, 2, 24, 16, odd[72:88]),
            )
            new = []
            for flat, state, m, lo, n, g in grads:
                rows = pl.ds(lo, n)
                flat[cb, m, rows, :] = g
                new.append(
                    advance(g, state[0, cb, m, rows, :], state[1, cb, m, rows, :], state[2, cb, m, rows, :], clip)[0]
                )
            first_half = jnp.concatenate(new[:4], axis=0)
            other = pltpu.roll(jnp.concatenate(new[4:] + [jnp.zeros((8, 128), F32)], axis=0), 64, 1)
            place = 3 + dz if dz else 0
            held_back[place, xs * 2] = jnp.where(low, first_half, other).astype(BF16)
            held_back[place, xs * 2 + 1] = jnp.where(low, other, first_half).astype(BF16)
            for m in range(4):
                pltpu.make_async_copy(flat_attn.at[cb, m], attn_out.at[:, cb, m, :], flat_sem.at[0]).start()
            for m in range(3):
                pltpu.make_async_copy(flat_mlp.at[cb, m], mlp_out.at[:, cb, m, :], flat_sem.at[1]).start()
            if dz:
                ret.send_a(dz, xs * 2)
                ret.send_a(dz, xs * 2 + 1)
            return carry

        lax.fori_loop(0, 4, one, 0)

    work(0)
    ret.pass_b(0)
    work(1)
    work(3)
    ret.pass_b(1)
    work(2)
    ret.pass_b(3)
    ret.pass_c(0)
    ret.pass_b(2)
    ret.pass_c(1)
    ret.pass_c(3)
    ret.pass_c(2)
    for d in range(1, 4):
        for xc in range(8):
            ret.take_c((y + d) % 4, xc)

    go.drain()
    ret.drain()
    for slot in range(3, 16):
        wait_for(sums.at[slot], sum_sent.at[slot])
    wait_for(flat_attn, flat_sem.at[0])
    wait_for(flat_mlp, flat_sem.at[1])


def run_exchange(attn_grads, mlp_grads, states):
    dma = pltpu.SemaphoreType.DMA
    any_spec = pl.BlockSpec(memory_space=pl.ANY)
    return pl.pallas_call(
        exchange_kernel,
        name="exchange",
        out_shape=(
            jax.ShapeDtypeStruct((16, 16, 4, 128), F32),
            jax.ShapeDtypeStruct((40, 16, 3, 128), F32),
            jax.ShapeDtypeStruct((8, 128), F32),
            jax.ShapeDtypeStruct((8, 8, ROWS, 128), BF16),
        ),
        in_specs=[any_spec] * 8,
        out_specs=(any_spec, any_spec, pl.BlockSpec(memory_space=pltpu.VMEM), any_spec),
        scratch_shapes=[
            pltpu.VMEM((2, 128, 512), F32),
            pltpu.VMEM((2, 128, 1280), F32),
            pltpu.VMEM((2, 512, 128), F32),
            pltpu.VMEM((2, 1288, 128), F32),
            pltpu.VMEM((7, 8, ROWS, 128), BF16),
            pltpu.VMEM((8, 8, ROWS, 128), BF16),
            pltpu.VMEM((7, 8, ROWS, 128), BF16),
            pltpu.VMEM((3, 16, 4, 16, 128), F32),
            pltpu.VMEM((3, 16, 3, 40, 128), F32),
            pltpu.VMEM((16, 4, 16, 128), F32),
            pltpu.VMEM((16, 3, 40, 128), F32),
            pltpu.VMEM((16, 8, 128), F32),
            dma((2,)),
            dma((2,)),
            dma((2,)),
            dma((16,)),
            dma((16,)),
            dma((4, 8)),
            dma((4, 8)),
            dma((4, 8)),
            dma,
            dma((4,)),
            dma,
            dma((4, 8)),
            dma((4, 8)),
            dma((4, 8)),
            dma,
            dma((4,)),
            dma,
        ],
        compiler_params=pltpu.CompilerParams(collective_id=0, has_side_effects=True, vmem_limit_bytes=32 << 20),
    )(attn_grads, mlp_grads, *states)


def rows_first(flat, rows):
    return flat.reshape(flat.shape[0], rows, 16, 128).transpose(1, 2, 0, 3)


def members_first(value):
    rows, _, members, _ = value.shape
    return value.transpose(2, 0, 1, 3).reshape(members, rows * D)


def per_device(
    attn_grads,
    mlp_grads,
    attn_master,
    attn_first,
    attn_second,
    attn_average,
    mlp_master,
    mlp_first,
    mlp_second,
    mlp_average,
):
    attn_states = [rows_first(v, 16) for v in (attn_master, attn_first, attn_second)]
    mlp_states = [rows_first(v, 40) for v in (mlp_master, mlp_first, mlp_second)]
    flat_attn, flat_mlp, clip, back = run_exchange(
        attn_grads.transpose(0, 2, 1), mlp_grads.transpose(0, 2, 1), attn_states + mlp_states
    )
    factor = clip[0, 0]
    outs = []
    for grads, master, first, second, average in (
        (members_first(flat_attn), attn_master, attn_first, attn_second, attn_average),
        (members_first(flat_mlp), mlp_master, mlp_first, mlp_second, mlp_average),
    ):
        master_new, first_new, second_new = advance(grads, master, first, second, factor)
        outs += [master_new, first_new, second_new, average_keep * average + (1.0 - average_keep) * master_new]

    chunks = back[:4].transpose(1, 0, 2, 3).reshape(32, ROWS, 128)
    swapped = lax.axis_index("shard") % 2 == 1
    left, right = chunks[:, :, :64], chunks[:, :, 64:]
    even = jnp.where(swapped, right, left)
    odd = jnp.where(swapped, left, right)
    attn_weights = jnp.stack(
        [
            even[:, 0:16].reshape(512, 64),
            odd[:, 0:16].reshape(512, 64),
            even[:, 16:32].reshape(512, 64),
            odd[:, 16:32].reshape(512, 64),
        ]
    )
    mlp_weights = jnp.stack(
        [
            even[:, 32:72].reshape(1280, 64),
            odd[:, 32:72].reshape(1280, 64),
            jnp.concatenate([even[:, 72:96], odd[:, 72:88]], axis=1).reshape(1280, 64),
        ]
    )
    return (*outs, attn_weights, mlp_weights)


def solution(mesh):
    whole = P(None, "tensor", "shard")
    flat = P(None, ("shard", "tensor"))
    return jax.shard_map(
        per_device,
        mesh=mesh,
        in_specs=(whole,) * 2 + (flat,) * 8,
        out_specs=(flat,) * 8 + (whole,) * 2,
        check_vma=False,
    )
```

```python
import functools

import jax
import jax.numpy as jnp
from jax import lax
from jax.experimental import pallas as pl
from jax.experimental.pallas import tpu as pltpu
from jax.sharding import PartitionSpec as P

D = 2048
STEP = 100
COUNT = 48234496

beta_one = 0.9
beta_two = 0.999
adam_eps = 1e-08
learn_rate = 0.01
decay_weight = 0.1
average_keep = 0.999
clip_level = 1.0

MESH = pl.DeviceIdType.MESH
ROWS = 96
F32 = jnp.float32
BF16 = jnp.bfloat16


def advance(grads, master, first, second, average, clip):
    clipped = clip * grads
    first_new = beta_one * first + (1.0 - beta_one) * clipped
    second_new = beta_two * second + (1.0 - beta_two) * clipped * clipped
    update = (first_new * (1.0 / (1.0 - beta_one**STEP))) / (
        jnp.sqrt(second_new * (1.0 / (1.0 - beta_two**STEP))) + adam_eps
    )
    master_new = master - learn_rate * (update + decay_weight * master)
    average_new = average_keep * average + (1.0 - average_keep) * master_new
    return master_new, first_new, second_new, average_new


def low_lanes(rows):
    return lax.broadcasted_iota(jnp.int32, (rows, 128), 1) < 64


def split_halves(p_zero, p_one):
    low = low_lanes(p_zero.shape[0])
    return jnp.where(low, p_zero, p_one), pltpu.roll(jnp.where(low, p_one, p_zero), 64, 1)


def position():
    s = lax.axis_index("shard")
    return s // 8, (s // 2) % 4, s % 2, lax.axis_index("tensor")


def device(z, x, c, y):
    return (z * 8 + x * 2 + c, y)


def wait_for(ref, sem):
    pltpu.make_async_copy(ref, ref, sem).wait()


OTHERS = [(dx, dc) for dx in range(4) for dc in range(2)][1:]
TURNS = (1, 3, 2, 0)
RING = (0, 1, 3, 2)


class Exchange:
    def __init__(self, forward, held, landed, a_recv, b_recv, c_recv, a_sent, b_sent, c_sent):
        self.held, self.landed = held, landed
        self.a_recv, self.b_recv, self.c_recv = a_recv, b_recv, c_recv
        self.a_sent, self.b_sent, self.c_sent = a_sent, b_sent, c_sent
        self.z, self.x, self.c, self.y = position()
        self.forward = forward
        self.a, self.b = (self.y, self.z) if forward else (self.z, self.y)
        self.mine = self.x * 2 + self.c

    def at(self, a, x, c, b):
        return device(b, x, c, a) if self.forward else device(a, x, c, b)

    def target(self, turn, dc):
        dx = TURNS[turn] if self.forward else (4 - TURNS[turn]) % 4
        return (self.x + dx) % 4, (self.c + dc) % 2

    def source(self, turn, dc):
        dx = TURNS[turn] if self.forward else (4 - TURNS[turn]) % 4
        return (self.x + 4 - dx) % 4, (self.c + dc) % 2

    def send_a(self, da, xc):
        pltpu.make_async_remote_copy(
            src_ref=self.held.at[3 + da, xc],
            dst_ref=self.held.at[da, xc],
            send_sem=self.a_sent,
            recv_sem=self.a_recv.at[da, xc],
            device_id=self.at((self.a + da) % 4, self.x, self.c, self.b),
            device_id_type=MESH,
        ).start()

    def origin(self, da):
        origin = (self.a + 4 - da) % 4
        return origin, jnp.where(origin == self.b, origin, 4 + origin)

    def pass_b(self, turn):
        for dc in range(2):
            x, c = self.target(turn, dc)
            xc = x * 2 + c
            for da in RING:
                origin, slot = self.origin(da)
                if da:
                    wait_for(self.held.at[da, xc], self.a_recv.at[da, xc])
                if TURNS[turn] or dc:
                    pltpu.make_async_remote_copy(
                        src_ref=self.held.at[da, xc],
                        dst_ref=self.landed.at[slot, self.mine],
                        send_sem=self.b_sent.at[da],
                        recv_sem=self.b_recv.at[origin, self.mine],
                        device_id=self.at(self.a, x, c, self.b),
                        device_id_type=MESH,
                    ).start()
                else:
                    pltpu.make_async_copy(
                        self.held.at[da, xc], self.landed.at[slot, xc], self.b_recv.at[origin, xc]
                    ).start()

    def pass_c(self, turn):
        for dc in range(2):
            x, c = self.source(turn, dc)
            xc = x * 2 + c
            for da in RING:
                origin, slot = self.origin(da)
                wait_for(self.landed.at[slot, xc], self.b_recv.at[origin, xc])

                @pl.when(origin != self.b)
                def _():
                    pltpu.make_async_remote_copy(
                        src_ref=self.landed.at[slot, xc],
                        dst_ref=self.landed.at[self.b, xc],
                        send_sem=self.c_sent,
                        recv_sem=self.c_recv.at[self.b, xc],
                        device_id=self.at(self.a, self.x, self.c, origin),
                        device_id_type=MESH,
                    ).start()

    def take_c(self, source, xc):
        wait_for(self.landed.at[source, xc], self.c_recv.at[source, xc])

    def drain(self):
        wait_for(self.held.at[pl.ds(4, 3)], self.a_sent)
        for da in range(4):
            wait_for(self.held.at[da, pl.ds(0, 7)], self.b_sent.at[da])
        wait_for(self.held.at[pl.ds(4, 3)], self.c_sent)


def exchange_kernel(
    attn_grads,
    mlp_grads,
    attn_master,
    attn_first,
    attn_second,
    attn_average,
    mlp_master,
    mlp_first,
    mlp_second,
    mlp_average,
    attn_master_new,
    attn_first_new,
    attn_second_new,
    attn_average_new,
    mlp_master_new,
    mlp_first_new,
    mlp_second_new,
    mlp_average_new,
    back,
    stack_attn,
    stack_mlp,
    turned_attn,
    turned_mlp,
    held,
    landed,
    held_back,
    state_attn,
    state_mlp,
    sums,
    grad_sem,
    state_sem,
    flat_sem,
    sum_recv,
    sum_sent,
    fa_recv,
    fb_recv,
    fc_recv,
    fa_sent,
    fb_sent,
    fc_sent,
    ra_recv,
    rb_recv,
    rc_recv,
    ra_sent,
    rb_sent,
    rc_sent,
):
    z, x, c, y = position()
    barrier = pltpu.get_barrier_semaphore()
    for d in range(1, 4):
        pl.semaphore_signal(barrier, inc=1, device_id=device(z, x, c, (y + d) % 4), device_id_type=MESH)
        pl.semaphore_signal(barrier, inc=1, device_id=device((z + d) % 4, x, c, y), device_id_type=MESH)
    for dx, dc in OTHERS:
        pl.semaphore_signal(barrier, inc=1, device_id=device(z, (x + dx) % 4, (c + dc) % 2, y), device_id_type=MESH)

    for pair in range(2):
        for i in range(2):
            half = pl.ds(pl.multiple_of(64 * ((i + c) % 2), 64), 64)
            pltpu.make_async_copy(attn_grads.at[2 * pair + i], stack_attn.at[pair, half, :], grad_sem.at[0]).start()
    for i in range(2):
        half = pl.ds(pl.multiple_of(64 * ((i + c) % 2), 64), 64)
        pltpu.make_async_copy(mlp_grads.at[i], stack_mlp.at[0, half, :], grad_sem.at[1]).start()
        pltpu.make_async_copy(mlp_grads.at[2], stack_mlp.at[1, pl.ds(64 * i, 64), :], grad_sem.at[1]).start()
    olds = (
        (attn_master, mlp_master),
        (attn_first, mlp_first),
        (attn_second, mlp_second),
        (attn_average, mlp_average),
    )
    for k, (attn, mlp) in enumerate(olds):

        def fetch(cb, carry, k=k, attn=attn, mlp=mlp):
            for m in range(4):
                pltpu.make_async_copy(attn.at[:, cb, m, :], state_attn.at[k, cb, m], state_sem.at[0]).start()
            for m in range(3):
                pltpu.make_async_copy(mlp.at[:, cb, m, :], state_mlp.at[k, cb, m], state_sem.at[1]).start()
            return carry

        lax.fori_loop(0, 16, fetch, 0)
    turned_mlp[1, pl.ds(1280, 8), :] = jnp.zeros((8, 128), F32)

    wait_for(stack_attn, grad_sem.at[0])
    wait_for(stack_mlp, grad_sem.at[1])

    total = jnp.zeros((8, 128), F32)
    for pair in range(2):
        for b in range(4):
            block = stack_attn[pair, :, b * 128 : (b + 1) * 128]
            total = total + jnp.sum((block * block).reshape(16, 8, 128), axis=0)
            turned_attn[pair, b * 128 : (b + 1) * 128, :] = block.T
    for b in range(10):
        block = stack_mlp[0, :, b * 128 : (b + 1) * 128]
        total = total + jnp.sum((block * block).reshape(16, 8, 128), axis=0)
        turned_mlp[0, b * 128 : (b + 1) * 128, :] = block.T
        block = stack_mlp[1, :, b * 128 : (b + 1) * 128]
        turned_mlp[1, b * 128 : (b + 1) * 128, :] = block.T
        block = block[:64]
        total = total + jnp.sum((block * block).reshape(8, 8, 128), axis=0)
    sums[0] = total

    straight = (low_lanes(24).astype(jnp.int32) + c) == 1

    def pack(xc, carry):
        for dest in range(4):
            j = xc * 4 + dest
            a_rows = pl.ds(pl.multiple_of(j * 16, 16), 16)
            m_rows = pl.ds(pl.multiple_of(j * 40, 8), 40)
            t_rows = pl.ds(pl.multiple_of(j * 40, 8), 24)
            u_rows = pl.ds(pl.multiple_of(j * 40 + 24, 8), 24)
            packed = jnp.concatenate(
                [
                    turned_attn[0, a_rows, :],
                    turned_attn[1, a_rows, :],
                    turned_mlp[0, m_rows, :],
                    jnp.where(straight, turned_mlp[1, t_rows, :], turned_mlp[1, u_rows, :]),
                ],
                axis=0,
            ).astype(BF16)
            da = (dest + 4 - y) % 4
            held[jnp.where(da == 0, 0, 3 + da), xc] = packed
        return carry

    lax.fori_loop(0, 8, pack, 0)

    pl.semaphore_wait(barrier, 13)

    def send_sum(src, slot, dev):
        pltpu.make_async_remote_copy(
            src_ref=sums.at[src],
            dst_ref=sums.at[slot],
            send_sem=sum_sent.at[slot],
            recv_sem=sum_recv.at[slot],
            device_id=dev,
            device_id_type=MESH,
        ).start()

    for d in range(1, 4):
        send_sum(0, 2 + d, device(z, x, c, (y + d) % 4))

    go = Exchange(True, held, landed, fa_recv, fb_recv, fc_recv, fa_sent, fb_sent, fc_sent)
    for turn in range(4):
        for dc in range(2):
            tx, tc = go.target(turn, dc)
            for da in RING[1:]:
                go.send_a(da, tx * 2 + tc)
    go.pass_b(0)

    for slot in range(3, 6):
        wait_for(sums.at[slot], sum_recv.at[slot])
    sums[1] = sums[0] + sums[3] + sums[4] + sums[5]
    for k, (dx, dc) in enumerate(OTHERS):
        send_sum(1, 6 + k, device(z, (x + dx) % 4, (c + dc) % 2, y))

    go.pass_b(1)
    go.pass_c(0)

    for slot in range(6, 13):
        wait_for(sums.at[slot], sum_recv.at[slot])
    value = sums[1]
    for slot in range(6, 13):
        value = value + sums[slot]
    sums[2] = value
    for d in range(1, 4):
        send_sum(2, 12 + d, device((z + d) % 4, x, c, y))

    go.pass_b(2)
    go.pass_c(1)
    go.pass_b(3)
    go.pass_c(2)

    for slot in range(13, 16):
        wait_for(sums.at[slot], sum_recv.at[slot])
    grand = jnp.sum(sums[2] + sums[13] + sums[14] + sums[15], keepdims=True)
    clip = jnp.minimum(1.0, clip_level / jnp.sqrt(grand / COUNT + 1e-06))

    wait_for(state_attn, state_sem.at[0])
    wait_for(state_mlp, state_sem.at[1])

    ret = Exchange(False, held_back, back, ra_recv, rb_recv, rc_recv, ra_sent, rb_sent, rc_sent)
    low = low_lanes(ROWS)

    def work(turn):
        xs, _ = go.source(turn, 0)

        def one(source, place, da):
            cb = source * 4 + xs
            even, odd = split_halves(landed[source, xs * 2].astype(F32), landed[source, xs * 2 + 1].astype(F32))
            pieces = (
                (state_attn, 0, 0, 16, even[0:16]),
                (state_attn, 2, 0, 16, even[16:32]),
                (state_mlp, 0, 0, 40, even[32:72]),
                (state_mlp, 2, 0, 24, even[72:96]),
                (state_attn, 1, 0, 16, odd[0:16]),
                (state_attn, 3, 0, 16, odd[16:32]),
                (state_mlp, 1, 0, 40, odd[32:72]),
                (state_mlp, 2, 24, 16, odd[72:88]),
            )
            new = []
            for state, m, lo, n, g in pieces:
                rows = pl.ds(lo, n)
                values = advance(g, *(state[k, cb, m, rows, :] for k in range(4)), clip)
                for k in range(4):
                    state[k, cb, m, rows, :] = values[k]
                new.append(values[0])
            first_half = jnp.concatenate(new[:4], axis=0)
            other = pltpu.roll(jnp.concatenate(new[4:] + [jnp.zeros((8, 128), F32)], axis=0), 64, 1)
            held_back[place, xs * 2] = jnp.where(low, first_half, other).astype(BF16)
            held_back[place, xs * 2 + 1] = jnp.where(low, other, first_half).astype(BF16)

        one(z, 0, 0)

        def distant(da, carry):
            source = (z + da) % 4
            for dc in range(2):
                go.take_c(source, xs * 2 + dc)
            one(source, 3 + da, da)
            for dc in range(2):
                ret.send_a(da, xs * 2 + dc)
            return carry

        lax.fori_loop(1, 4, distant, 0)

    news = (
        (attn_master_new, mlp_master_new),
        (attn_first_new, mlp_first_new),
        (attn_second_new, mlp_second_new),
        (attn_average_new, mlp_average_new),
    )

    def store(turn):
        xs, _ = go.source(turn, 0)

        def one(zs, carry):
            cb = zs * 4 + xs
            for k, (attn, mlp) in enumerate(news):
                for m in range(4):
                    pltpu.make_async_copy(state_attn.at[k, cb, m], attn.at[:, cb, m, :], flat_sem.at[0]).start()
                for m in range(3):
                    pltpu.make_async_copy(state_mlp.at[k, cb, m], mlp.at[:, cb, m, :], flat_sem.at[1]).start()
            return carry

        lax.fori_loop(0, 4, one, 0)

    work(0)
    work(1)
    ret.pass_b(0)
    go.pass_c(3)
    work(2)
    ret.pass_b(1)
    ret.pass_c(0)
    work(3)
    ret.pass_b(2)
    ret.pass_c(1)
    ret.pass_b(3)
    store(0)
    ret.pass_c(2)
    store(1)
    ret.pass_c(3)
    store(2)
    store(3)
    for d in range(1, 4):
        for xc in range(8):
            ret.take_c((y + d) % 4, xc)

    go.drain()
    ret.drain()
    for slot in range(3, 16):
        wait_for(sums.at[slot], sum_sent.at[slot])
    wait_for(state_attn, flat_sem.at[0])
    wait_for(state_mlp, flat_sem.at[1])


def run_exchange(args):
    dma = pltpu.SemaphoreType.DMA
    any_spec = pl.BlockSpec(memory_space=pl.ANY)
    return pl.pallas_call(
        exchange_kernel,
        name="exchange",
        out_shape=(
            *[jax.ShapeDtypeStruct((16, 16, 4, 128), F32)] * 4,
            *[jax.ShapeDtypeStruct((40, 16, 3, 128), F32)] * 4,
            jax.ShapeDtypeStruct((8, 8, ROWS, 128), BF16),
        ),
        in_specs=[pl.BlockSpec(memory_space=pltpu.HBM)] * 10,
        out_specs=[any_spec] * 9,
        scratch_shapes=[
            pltpu.VMEM((2, 128, 512), F32),
            pltpu.VMEM((2, 128, 1280), F32),
            pltpu.VMEM((2, 512, 128), F32),
            pltpu.VMEM((2, 1288, 128), F32),
            pltpu.VMEM((7, 8, ROWS, 128), BF16),
            pltpu.VMEM((8, 8, ROWS, 128), BF16),
            pltpu.VMEM((7, 8, ROWS, 128), BF16),
            pltpu.VMEM((4, 16, 4, 16, 128), F32),
            pltpu.VMEM((4, 16, 3, 40, 128), F32),
            pltpu.VMEM((16, 8, 128), F32),
            dma((2,)),
            dma((2,)),
            dma((2,)),
            dma((16,)),
            dma((16,)),
            dma((4, 8)),
            dma((4, 8)),
            dma((4, 8)),
            dma,
            dma((4,)),
            dma,
            dma((4, 8)),
            dma((4, 8)),
            dma((4, 8)),
            dma,
            dma((4,)),
            dma,
        ],
        compiler_params=pltpu.CompilerParams(collective_id=0, has_side_effects=True, vmem_limit_bytes=32 << 20),
    )(*args)


def finish_kernel(*refs):
    news, back, outs = refs[:8], refs[8], refs[9:17]
    attn_weights, mlp_weights, turned_attn, turned_mlp, sem = refs[17:]
    c = lax.axis_index("shard") % 2
    for k in range(8):
        pltpu.make_async_copy(news[k], outs[k], sem.at[k]).start()
    turned_mlp[1, pl.ds(1280, 8), :] = jnp.zeros((8, 128), F32)

    def unpack(xc, carry):
        for src in range(4):
            j = xc * 4 + src
            chunk = back[src, xc].astype(F32)
            turned_attn[0, pl.ds(pl.multiple_of(j * 16, 16), 16), :] = chunk[0:16]
            turned_attn[1, pl.ds(pl.multiple_of(j * 16, 16), 16), :] = chunk[16:32]
            turned_mlp[0, pl.ds(pl.multiple_of(j * 40, 8), 40), :] = chunk[32:72]
            tail = chunk[72:96]
            turn = pltpu.roll(tail, 64, 1)
            straight = lax.broadcast(c, (24, 128)) == 0
            turned_mlp[1, pl.ds(pl.multiple_of(j * 40, 8), 24), :] = jnp.where(straight, tail, turn)
            turned_mlp[1, pl.ds(pl.multiple_of(j * 40 + 24, 8), 16), :] = jnp.where(straight, turn, tail)[:16]
        return carry

    lax.fori_loop(0, 8, unpack, 0)
    for b in range(4):
        cols = slice(b * 128, (b + 1) * 128)
        for pair in range(2):
            block = turned_attn[pair, cols, :].T.astype(BF16)
            for half in range(2):
                attn_weights[2 * pair + (half + c) % 2, :, cols] = block[64 * half : 64 * half + 64]
    for b in range(10):
        cols = slice(b * 128, (b + 1) * 128)
        block = turned_mlp[0, cols, :].T.astype(BF16)
        for half in range(2):
            mlp_weights[(half + c) % 2, :, cols] = block[64 * half : 64 * half + 64]
        mlp_weights[2, :, cols] = turned_mlp[1, cols, :].T[:64].astype(BF16)
    for k in range(8):
        pltpu.make_async_copy(news[k], outs[k], sem.at[k]).wait()


def run_finish(news, back):
    any_spec = pl.BlockSpec(memory_space=pl.ANY)
    vmem = pl.BlockSpec(memory_space=pltpu.VMEM)
    return pl.pallas_call(
        finish_kernel,
        name="finish",
        out_shape=(
            *[jax.ShapeDtypeStruct(v.shape, F32) for v in news],
            jax.ShapeDtypeStruct((4, 64, 512), BF16),
            jax.ShapeDtypeStruct((3, 64, 1280), BF16),
        ),
        in_specs=[any_spec] * 8 + [vmem],
        out_specs=[pl.BlockSpec(memory_space=pltpu.HBM)] * 8 + [vmem] * 2,
        scratch_shapes=[
            pltpu.VMEM((2, 512, 128), F32),
            pltpu.VMEM((2, 1288, 128), F32),
            pltpu.SemaphoreType.DMA((8,)),
        ],
        compiler_params=pltpu.CompilerParams(vmem_limit_bytes=24 << 20),
    )(*news, back)


def rows_first(flat, rows):
    return flat.reshape(flat.shape[0], rows, 16, 128).transpose(1, 2, 0, 3)


def members_first(value):
    rows, _, members, _ = value.shape
    return value.transpose(2, 0, 1, 3).reshape(members, rows * D)


def per_device(attn_grads, mlp_grads, *states):
    states = [rows_first(v, 16) for v in states[:4]] + [rows_first(v, 40) for v in states[4:]]
    args = [attn_grads.transpose(0, 2, 1), mlp_grads.transpose(0, 2, 1), *states]
    *news, back = run_exchange([pltpu.with_memory_space_constraint(v, pltpu.HBM) for v in args])
    *outs, attn_weights, mlp_weights = run_finish(news, back)
    outs = [members_first(v) for v in outs]
    return (*outs, attn_weights.transpose(0, 2, 1), mlp_weights.transpose(0, 2, 1))


def solution(mesh):
    whole = P(None, "tensor", "shard")
    flat = P(None, ("shard", "tensor"))
    return jax.shard_map(
        per_device,
        mesh=mesh,
        in_specs=(whole,) * 2 + (flat,) * 8,
        out_specs=(flat,) * 8 + (whole,) * 2,
        check_vma=False,
    )
```

```python
import functools

import jax
import jax.numpy as jnp
from jax import lax
from jax.experimental import pallas as pl
from jax.experimental.pallas import tpu as pltpu
from jax.sharding import PartitionSpec as P

D = 2048
STEP = 100
COUNT = 48234496

beta_one = 0.9
beta_two = 0.999
adam_eps = 1e-08
learn_rate = 0.01
decay_weight = 0.1
average_keep = 0.999
clip_level = 1.0

MESH = pl.DeviceIdType.MESH
ROWS = 96
F32 = jnp.float32
BF16 = jnp.bfloat16


def advance(grads, master, first, second, average, clip):
    clipped = clip * grads
    first_new = beta_one * first + (1.0 - beta_one) * clipped
    second_new = beta_two * second + (1.0 - beta_two) * clipped * clipped
    update = (first_new * (1.0 / (1.0 - beta_one**STEP))) / (
        jnp.sqrt(second_new * (1.0 / (1.0 - beta_two**STEP))) + adam_eps
    )
    master_new = master - learn_rate * (update + decay_weight * master)
    average_new = average_keep * average + (1.0 - average_keep) * master_new
    return master_new, first_new, second_new, average_new


def low_lanes(rows):
    return lax.broadcasted_iota(jnp.int32, (rows, 128), 1) < 64


def split_halves(p_zero, p_one):
    low = low_lanes(p_zero.shape[0])
    return jnp.where(low, p_zero, p_one), pltpu.roll(jnp.where(low, p_one, p_zero), 64, 1)


def position():
    s = lax.axis_index("shard")
    return s // 8, (s // 2) % 4, s % 2, lax.axis_index("tensor")


def device(z, x, c, y):
    return (z * 8 + x * 2 + c, y)


def wait_for(ref, sem):
    pltpu.make_async_copy(ref, ref, sem).wait()


PLANE = [(dx, dc, dy) for dy in range(4) for dx in range(4) for dc in range(2)][1:]


def send(src, dst, sent, received, target):
    pltpu.make_async_remote_copy(
        src_ref=src, dst_ref=dst, send_sem=sent, recv_sem=received, device_id=target, device_id_type=MESH
    ).start()


def exchange_kernel(
    attn_grads,
    mlp_grads,
    attn_master,
    attn_first,
    attn_second,
    attn_average,
    mlp_master,
    mlp_first,
    mlp_second,
    mlp_average,
    attn_master_new,
    attn_first_new,
    attn_second_new,
    attn_average_new,
    mlp_master_new,
    mlp_first_new,
    mlp_second_new,
    mlp_average_new,
    back,
    stack_attn,
    stack_mlp,
    turned_attn,
    turned_mlp,
    held,
    landed,
    held_back,
    state_attn,
    state_mlp,
    sums,
    grad_sem,
    state_sem,
    flat_sem,
    sum_recv,
    sum_sent,
    plane_recv,
    ring_recv,
    plane_sent,
    ring_sent,
    back_ring_recv,
    back_plane_recv,
    back_ring_sent,
    back_plane_sent,
):
    z, x, c, y = position()
    mine = x * 2 + c
    barrier = pltpu.get_barrier_semaphore()

    for pair in range(2):
        for i in range(2):
            half = pl.ds(pl.multiple_of(64 * ((i + c) % 2), 64), 64)
            pltpu.make_async_copy(attn_grads.at[2 * pair + i], stack_attn.at[pair, half, :], grad_sem.at[0]).start()
    for i in range(2):
        half = pl.ds(pl.multiple_of(64 * ((i + c) % 2), 64), 64)
        pltpu.make_async_copy(mlp_grads.at[i], stack_mlp.at[0, half, :], grad_sem.at[1]).start()
        pltpu.make_async_copy(mlp_grads.at[2], stack_mlp.at[1, pl.ds(64 * i, 64), :], grad_sem.at[1]).start()
    for dx, dc, dy in PLANE:
        pl.semaphore_signal(
            barrier, inc=1, device_id=device(z, (x + dx) % 4, (c + dc) % 2, (y + dy) % 4), device_id_type=MESH
        )
    for dz in range(1, 4):
        pl.semaphore_signal(barrier, inc=1, device_id=device((z + dz) % 4, x, c, y), device_id_type=MESH)
    turned_mlp[1, pl.ds(1280, 8), :] = jnp.zeros((8, 128), F32)

    wait_for(stack_attn, grad_sem.at[0])
    wait_for(stack_mlp, grad_sem.at[1])

    total = jnp.zeros((8, 128), F32)
    for pair in range(2):
        for b in range(4):
            block = stack_attn[pair, :, b * 128 : (b + 1) * 128]
            total = total + jnp.sum((block * block).reshape(16, 8, 128), axis=0)
            turned_attn[pair, b * 128 : (b + 1) * 128, :] = block.T
    for b in range(10):
        block = stack_mlp[0, :, b * 128 : (b + 1) * 128]
        total = total + jnp.sum((block * block).reshape(16, 8, 128), axis=0)
        turned_mlp[0, b * 128 : (b + 1) * 128, :] = block.T
        block = stack_mlp[1, :, b * 128 : (b + 1) * 128]
        turned_mlp[1, b * 128 : (b + 1) * 128, :] = block.T
        block = block[:64]
        total = total + jnp.sum((block * block).reshape(8, 8, 128), axis=0)
    sums[0] = jnp.sum(total, axis=0, keepdims=True)

    straight = (low_lanes(24).astype(jnp.int32) + c) == 1

    def pack(xc, carry):
        for dest in range(4):
            j = xc * 4 + dest
            a_rows = pl.ds(pl.multiple_of(j * 16, 16), 16)
            m_rows = pl.ds(pl.multiple_of(j * 40, 8), 40)
            t_rows = pl.ds(pl.multiple_of(j * 40, 8), 24)
            u_rows = pl.ds(pl.multiple_of(j * 40 + 24, 8), 24)
            packed = jnp.concatenate(
                [
                    turned_attn[0, a_rows, :],
                    turned_attn[1, a_rows, :],
                    turned_mlp[0, m_rows, :],
                    jnp.where(straight, turned_mlp[1, t_rows, :], turned_mlp[1, u_rows, :]),
                ],
                axis=0,
            ).astype(BF16)
            held[dest, xc] = packed
        return carry

    lax.fori_loop(0, 8, pack, 0)

    pl.semaphore_wait(barrier, len(PLANE) + 3)

    for k, (dx, dc, dy) in enumerate(PLANE):
        to = device(z, (x + dx) % 4, (c + dc) % 2, (y + dy) % 4)
        send(sums.at[0], sums.at[2 + k], sum_sent.at[0], sum_recv.at[2 + k], to)

    def plane_slot(origin):
        return jnp.where(origin == z, origin, 4 + origin)

    for step in range(4):
        for dy in range(4):
            dx, to_y = (step + dy) % 4, (y + dy) % 4
            for dc in range(2):
                to_x, to_c = (x + dx) % 4, (c + dc) % 2
                src = held.at[to_y, to_x * 2 + to_c]
                dst = landed.at[plane_slot(y), mine]
                if dx or dy or dc:
                    send(src, dst, plane_sent.at[min(dy, 1)], plane_recv.at[y, mine], device(z, to_x, to_c, to_y))
                else:
                    pltpu.make_async_copy(src, dst, plane_recv.at[y, mine]).start()

    olds = (
        (attn_master, mlp_master),
        (attn_first, mlp_first),
        (attn_second, mlp_second),
        (attn_average, mlp_average),
    )
    for k, (attn, mlp) in enumerate(olds):

        def fetch(cb, carry, k=k, attn=attn, mlp=mlp):
            for m in range(4):
                pltpu.make_async_copy(attn.at[:, cb, m, :], state_attn.at[k, cb, m], state_sem.at[0]).start()
            for m in range(3):
                pltpu.make_async_copy(mlp.at[:, cb, m, :], state_mlp.at[k, cb, m], state_sem.at[1]).start()
            return carry

        lax.fori_loop(0, 16, fetch, 0)

    def ring(step):
        for dy in range(4):
            dx, from_y = (step + dy) % 4, (y + 4 - dy) % 4
            slot = plane_slot(from_y)
            for dc in range(2):
                xc = (x + 4 - dx) % 4 * 2 + (c + dc) % 2
                wait_for(landed.at[slot, xc], plane_recv.at[from_y, xc])

                @pl.when(from_y != z)
                def _():
                    send(landed.at[slot, xc], landed.at[z, xc], ring_sent, ring_recv.at[z, xc], device(from_y, x, c, y))

    ring(0)
    value = sums[0]
    for k in range(len(PLANE)):
        wait_for(sums.at[2 + k], sum_recv.at[2 + k])
        value = value + sums[2 + k]
    sums[1] = value
    ring(1)
    ahead = 2 + len(PLANE)
    for dz in range(1, 4):
        send(sums.at[1], sums.at[ahead + dz - 1], sum_sent.at[1], sum_recv.at[ahead + dz - 1], device((z + dz) % 4, x, c, y))
    ring(2)
    ring(3)
    value = sums[1]
    for dz in range(3):
        wait_for(sums.at[ahead + dz], sum_recv.at[ahead + dz])
        value = value + sums[ahead + dz]
    grand = jnp.sum(value, keepdims=True)
    clip = jnp.minimum(1.0, clip_level / jnp.sqrt(grand / COUNT + 1e-06))

    wait_for(state_attn, state_sem.at[0])
    wait_for(state_mlp, state_sem.at[1])

    low = low_lanes(ROWS)

    def column(step, from_z):
        return (x + 8 - (step + y + 4 - from_z) % 4) % 4

    def work(step):
        xs = (x + 4 - (step + y + 4 - z) % 4) % 4

        def one(source, place):
            cb = source * 4 + xs
            even, odd = split_halves(landed[source, xs * 2].astype(F32), landed[source, xs * 2 + 1].astype(F32))
            pieces = (
                (state_attn, 0, 0, 16, even[0:16]),
                (state_attn, 2, 0, 16, even[16:32]),
                (state_mlp, 0, 0, 40, even[32:72]),
                (state_mlp, 2, 0, 24, even[72:96]),
                (state_attn, 1, 0, 16, odd[0:16]),
                (state_attn, 3, 0, 16, odd[16:32]),
                (state_mlp, 1, 0, 40, odd[32:72]),
                (state_mlp, 2, 24, 16, odd[72:88]),
            )
            new = []
            for state, m, lo, n, g in pieces:
                rows = pl.ds(lo, n)
                values = advance(g, *(state[k, cb, m, rows, :] for k in range(4)), clip)
                for k in range(4):
                    state[k, cb, m, rows, :] = values[k]
                new.append(values[0])
            first_half = jnp.concatenate(new[:4], axis=0)
            other = pltpu.roll(jnp.concatenate(new[4:] + [jnp.zeros((8, 128), F32)], axis=0), 64, 1)
            held_back[place, xs * 2] = jnp.where(low, first_half, other).astype(BF16)
            held_back[place, xs * 2 + 1] = jnp.where(low, other, first_half).astype(BF16)

        def pass_on(dz):
            for dc in range(2):
                xc = xs * 2 + dc
                send(
                    held_back.at[3 + dz, xc],
                    held_back.at[dz, xc],
                    back_ring_sent,
                    back_ring_recv.at[dz, xc],
                    device((z + dz) % 4, x, c, y),
                )

        def distant(dz, carry):
            source = (z + dz) % 4
            for dc in range(2):
                wait_for(landed.at[source, xs * 2 + dc], ring_recv.at[source, xs * 2 + dc])
            one(source, 3 + dz)

            @pl.when(dz > 1)
            def _():
                pass_on(dz - 1)

            return carry

        lax.fori_loop(1, 4, distant, 0)
        one(z, 0)
        pass_on(3)

    def spread(step):
        for dz in range(4):
            from_z = (z + 4 - dz) % 4
            xs = column(step, from_z)
            for dc in range(2):
                xc = xs * 2 + dc
                src, dst, received = held_back.at[dz, xc], back.at[y, mine], back_plane_recv.at[y, mine]
                if dz:
                    wait_for(src, back_ring_recv.at[dz, xc])
                here = jnp.logical_and(xc == mine, from_z == y)

                @pl.when(here)
                def _():
                    pltpu.make_async_copy(src, dst, received).start()

                @pl.when(jnp.logical_not(here))
                def _():
                    send(src, dst, back_plane_sent.at[jnp.where(from_z == y, 0, 1)], received, device(z, xs, dc, from_z))

    news = (
        (attn_master_new, mlp_master_new),
        (attn_first_new, mlp_first_new),
        (attn_second_new, mlp_second_new),
        (attn_average_new, mlp_average_new),
    )

    def store(step):
        xs = (x + 4 - (step + y + 4 - z) % 4) % 4

        def one(zs, carry):
            cb = zs * 4 + xs
            for k, (attn, mlp) in enumerate(news):
                for m in range(4):
                    pltpu.make_async_copy(state_attn.at[k, cb, m], attn.at[:, cb, m, :], flat_sem.at[0]).start()
                for m in range(3):
                    pltpu.make_async_copy(state_mlp.at[k, cb, m], mlp.at[:, cb, m, :], flat_sem.at[1]).start()
            return carry

        lax.fori_loop(0, 4, one, 0)

    work(0)
    work(1)
    spread(0)
    work(2)
    spread(1)
    work(3)
    spread(2)
    store(0)
    spread(3)
    store(1)
    store(2)
    store(3)
    for src in range(4):
        for xc in range(8):
            wait_for(back.at[src, xc], back_plane_recv.at[src, xc])

    wait_for(sums.at[pl.ds(2, len(PLANE))], sum_sent.at[0])
    wait_for(sums.at[pl.ds(2, 3)], sum_sent.at[1])
    wait_for(landed.at[pl.ds(0, 3)], ring_sent)
    wait_for(landed.at[pl.ds(0, 3)], back_ring_sent)
    for sem in (plane_sent, back_plane_sent):
        wait_for(landed.at[0, pl.ds(0, 7)], sem.at[0])
        wait_for(landed.at[pl.ds(0, 3)], sem.at[1])
    wait_for(state_attn, flat_sem.at[0])
    wait_for(state_mlp, flat_sem.at[1])


def run_exchange(args):
    dma = pltpu.SemaphoreType.DMA
    any_spec = pl.BlockSpec(memory_space=pl.ANY)
    return pl.pallas_call(
        exchange_kernel,
        name="exchange",
        out_shape=(
            *[jax.ShapeDtypeStruct((16, 16, 4, 128), F32)] * 4,
            *[jax.ShapeDtypeStruct((40, 16, 3, 128), F32)] * 4,
            jax.ShapeDtypeStruct((4, 8, ROWS, 128), BF16),
        ),
        in_specs=[pl.BlockSpec(memory_space=pltpu.HBM)] * 10,
        out_specs=[any_spec] * 9,
        scratch_shapes=[
            pltpu.VMEM((2, 128, 512), F32),
            pltpu.VMEM((2, 128, 1280), F32),
            pltpu.VMEM((2, 512, 128), F32),
            pltpu.VMEM((2, 1288, 128), F32),
            pltpu.VMEM((4, 8, ROWS, 128), BF16),
            pltpu.VMEM((8, 8, ROWS, 128), BF16),
            pltpu.VMEM((7, 8, ROWS, 128), BF16),
            pltpu.VMEM((4, 16, 4, 16, 128), F32),
            pltpu.VMEM((4, 16, 3, 40, 128), F32),
            pltpu.VMEM((36, 1, 128), F32),
            dma((2,)),
            dma((2,)),
            dma((2,)),
            dma((36,)),
            dma((2,)),
            dma((4, 8)),
            dma((4, 8)),
            dma((2,)),
            dma,
            dma((4, 8)),
            dma((4, 8)),
            dma,
            dma((2,)),
        ],
        compiler_params=pltpu.CompilerParams(collective_id=0, has_side_effects=True, vmem_limit_bytes=32 << 20),
    )(*args)


def finish_kernel(*refs):
    news, back, outs = refs[:8], refs[8], refs[9:17]
    attn_weights, mlp_weights, turned_attn, turned_mlp, sem = refs[17:]
    c = lax.axis_index("shard") % 2
    for k in range(8):
        pltpu.make_async_copy(news[k], outs[k], sem.at[k]).start()
    turned_mlp[1, pl.ds(1280, 8), :] = jnp.zeros((8, 128), F32)

    def unpack(xc, carry):
        for src in range(4):
            j = xc * 4 + src
            chunk = back[src, xc].astype(F32)
            turned_attn[0, pl.ds(pl.multiple_of(j * 16, 16), 16), :] = chunk[0:16]
            turned_attn[1, pl.ds(pl.multiple_of(j * 16, 16), 16), :] = chunk[16:32]
            turned_mlp[0, pl.ds(pl.multiple_of(j * 40, 8), 40), :] = chunk[32:72]
            tail = chunk[72:96]
            turn = pltpu.roll(tail, 64, 1)
            straight = lax.broadcast(c, (24, 128)) == 0
            turned_mlp[1, pl.ds(pl.multiple_of(j * 40, 8), 24), :] = jnp.where(straight, tail, turn)
            turned_mlp[1, pl.ds(pl.multiple_of(j * 40 + 24, 8), 16), :] = jnp.where(straight, turn, tail)[:16]
        return carry

    lax.fori_loop(0, 8, unpack, 0)
    for b in range(4):
        cols = slice(b * 128, (b + 1) * 128)
        for pair in range(2):
            block = turned_attn[pair, cols, :].T.astype(BF16)
            for half in range(2):
                attn_weights[2 * pair + (half + c) % 2, :, cols] = block[64 * half : 64 * half + 64]
    for b in range(10):
        cols = slice(b * 128, (b + 1) * 128)
        block = turned_mlp[0, cols, :].T.astype(BF16)
        for half in range(2):
            mlp_weights[(half + c) % 2, :, cols] = block[64 * half : 64 * half + 64]
        mlp_weights[2, :, cols] = turned_mlp[1, cols, :].T[:64].astype(BF16)
    for k in range(8):
        pltpu.make_async_copy(news[k], outs[k], sem.at[k]).wait()


def run_finish(news, back):
    any_spec = pl.BlockSpec(memory_space=pl.ANY)
    vmem = pl.BlockSpec(memory_space=pltpu.VMEM)
    return pl.pallas_call(
        finish_kernel,
        name="finish",
        out_shape=(
            *[jax.ShapeDtypeStruct(v.shape, F32) for v in news],
            jax.ShapeDtypeStruct((4, 64, 512), BF16),
            jax.ShapeDtypeStruct((3, 64, 1280), BF16),
        ),
        in_specs=[any_spec] * 8 + [vmem],
        out_specs=[pl.BlockSpec(memory_space=pltpu.HBM)] * 8 + [vmem] * 2,
        scratch_shapes=[
            pltpu.VMEM((2, 512, 128), F32),
            pltpu.VMEM((2, 1288, 128), F32),
            pltpu.SemaphoreType.DMA((8,)),
        ],
        compiler_params=pltpu.CompilerParams(vmem_limit_bytes=24 << 20),
    )(*news, back)


def rows_first(flat, rows):
    return flat.reshape(flat.shape[0], rows, 16, 128).transpose(1, 2, 0, 3)


def members_first(value):
    rows, _, members, _ = value.shape
    return value.transpose(2, 0, 1, 3).reshape(members, rows * D)


def per_device(attn_grads, mlp_grads, *states):
    states = [rows_first(v, 16) for v in states[:4]] + [rows_first(v, 40) for v in states[4:]]
    args = [attn_grads.transpose(0, 2, 1), mlp_grads.transpose(0, 2, 1), *states]
    *news, back = run_exchange([pltpu.with_memory_space_constraint(v, pltpu.HBM) for v in args])
    *outs, attn_weights, mlp_weights = run_finish(news, back)
    outs = [members_first(v) for v in outs]
    return (*outs, attn_weights.transpose(0, 2, 1), mlp_weights.transpose(0, 2, 1))


def solution(mesh):
    whole = P(None, "tensor", "shard")
    flat = P(None, ("shard", "tensor"))
    return jax.shard_map(
        per_device,
        mesh=mesh,
        in_specs=(whole,) * 2 + (flat,) * 8,
        out_specs=(flat,) * 8 + (whole,) * 2,
        check_vma=False,
    )
```

```python
import functools

import jax
import jax.numpy as jnp
from jax import lax
from jax.experimental import pallas as pl
from jax.experimental.pallas import tpu as pltpu
from jax.sharding import PartitionSpec as P

D = 2048
STEP = 100
COUNT = 48234496

beta_one = 0.9
beta_two = 0.999
adam_eps = 1e-08
learn_rate = 0.01
decay_weight = 0.1
average_keep = 0.999
clip_level = 1.0

MESH = pl.DeviceIdType.MESH
ROWS = 96
F32 = jnp.float32
BF16 = jnp.bfloat16


def advance(grads, master, first, second, average, clip):
    clipped = clip * grads
    first_new = beta_one * first + (1.0 - beta_one) * clipped
    second_new = beta_two * second + (1.0 - beta_two) * clipped * clipped
    update = (first_new * (1.0 / (1.0 - beta_one**STEP))) / (
        jnp.sqrt(second_new * (1.0 / (1.0 - beta_two**STEP))) + adam_eps
    )
    master_new = master - learn_rate * (update + decay_weight * master)
    average_new = average_keep * average + (1.0 - average_keep) * master_new
    return master_new, first_new, second_new, average_new


def low_lanes(rows):
    return lax.broadcasted_iota(jnp.int32, (rows, 128), 1) < 64


def split_halves(p_zero, p_one):
    low = low_lanes(p_zero.shape[0])
    return jnp.where(low, p_zero, p_one), pltpu.roll(jnp.where(low, p_one, p_zero), 64, 1)


def position():
    s = lax.axis_index("shard")
    return s // 8, (s // 2) % 4, s % 2, lax.axis_index("tensor")


def device(z, x, c, y):
    return (z * 8 + x * 2 + c, y)


def wait_for(ref, sem):
    pltpu.make_async_copy(ref, ref, sem).wait()


PLANE = [(dx, dc, dz) for dz in range(4) for dx in range(4) for dc in range(2)][1:]


def send(src, dst, sent, received, target):
    pltpu.make_async_remote_copy(
        src_ref=src, dst_ref=dst, send_sem=sent, recv_sem=received, device_id=target, device_id_type=MESH
    ).start()


def exchange_kernel(
    attn_grads,
    mlp_grads,
    attn_master,
    attn_first,
    attn_second,
    attn_average,
    mlp_master,
    mlp_first,
    mlp_second,
    mlp_average,
    attn_master_new,
    attn_first_new,
    attn_second_new,
    attn_average_new,
    mlp_master_new,
    mlp_first_new,
    mlp_second_new,
    mlp_average_new,
    back,
    stack_attn,
    stack_mlp,
    turned_attn,
    turned_mlp,
    held,
    landed,
    held_back,
    relay,
    state_attn,
    state_mlp,
    sums,
    grad_sem,
    state_sem,
    flat_sem,
    sum_recv,
    sum_sent,
    grad_recv,
    grad_sent,
    back_ring_recv,
    back_plane_recv,
    back_ring_sent,
    back_plane_sent,
):
    z, x, c, y = position()
    mine = x * 2 + c
    barrier = pltpu.get_barrier_semaphore()

    for pair in range(2):
        for i in range(2):
            half = pl.ds(pl.multiple_of(64 * ((i + c) % 2), 64), 64)
            pltpu.make_async_copy(attn_grads.at[2 * pair + i], stack_attn.at[pair, half, :], grad_sem.at[0]).start()
    for i in range(2):
        half = pl.ds(pl.multiple_of(64 * ((i + c) % 2), 64), 64)
        pltpu.make_async_copy(mlp_grads.at[i], stack_mlp.at[0, half, :], grad_sem.at[1]).start()
        pltpu.make_async_copy(mlp_grads.at[2], stack_mlp.at[1, pl.ds(64 * i, 64), :], grad_sem.at[1]).start()
    def announce(to):
        pl.semaphore_signal(barrier, inc=1, device_id=to, device_id_type=MESH)

    for dz in range(4):
        for dx in range(4):
            for dc in range(2):
                to = device((z + dz) % 4, (x + dx) % 4, (c + dc) % 2, z)
                if dz or dx or dc:
                    announce(to)
                else:

                    @pl.when(y != z)
                    def _():
                        announce(to)

    for dx, dc, dz in PLANE:
        announce(device((z + dz) % 4, (x + dx) % 4, (c + dc) % 2, y))
    for dy in range(1, 4):
        announce(device(z, x, c, (y + dy) % 4))
    turned_mlp[1, pl.ds(1280, 8), :] = jnp.zeros((8, 128), F32)

    wait_for(stack_attn, grad_sem.at[0])
    wait_for(stack_mlp, grad_sem.at[1])

    total = jnp.zeros((8, 128), F32)
    for pair in range(2):
        for b in range(4):
            block = stack_attn[pair, :, b * 128 : (b + 1) * 128]
            total = total + jnp.sum((block * block).reshape(16, 8, 128), axis=0)
            turned_attn[pair, b * 128 : (b + 1) * 128, :] = block.T
    for b in range(10):
        block = stack_mlp[0, :, b * 128 : (b + 1) * 128]
        total = total + jnp.sum((block * block).reshape(16, 8, 128), axis=0)
        turned_mlp[0, b * 128 : (b + 1) * 128, :] = block.T
        block = stack_mlp[1, :, b * 128 : (b + 1) * 128]
        turned_mlp[1, b * 128 : (b + 1) * 128, :] = block.T
        block = block[:64]
        total = total + jnp.sum((block * block).reshape(8, 8, 128), axis=0)
    sums[0] = jnp.sum(total, axis=0, keepdims=True)

    straight = (low_lanes(24).astype(jnp.int32) + c) == 1

    def pack(xc, carry):
        for dest in range(4):
            j = xc * 4 + dest
            a_rows = pl.ds(pl.multiple_of(j * 16, 16), 16)
            m_rows = pl.ds(pl.multiple_of(j * 40, 8), 40)
            t_rows = pl.ds(pl.multiple_of(j * 40, 8), 24)
            u_rows = pl.ds(pl.multiple_of(j * 40 + 24, 8), 24)
            packed = jnp.concatenate(
                [
                    turned_attn[0, a_rows, :],
                    turned_attn[1, a_rows, :],
                    turned_mlp[0, m_rows, :],
                    jnp.where(straight, turned_mlp[1, t_rows, :], turned_mlp[1, u_rows, :]),
                ],
                axis=0,
            ).astype(BF16)
            held[dest, xc] = packed
        return carry

    lax.fori_loop(0, 8, pack, 0)

    pl.semaphore_wait(barrier, jnp.where(y == z, 31, 32) + len(PLANE) + 3)

    for k, (dx, dc, dz) in enumerate(PLANE):
        to = device((z + dz) % 4, (x + dx) % 4, (c + dc) % 2, y)
        send(sums.at[0], sums.at[2 + k], sum_sent.at[0], sum_recv.at[2 + k], to)

    alone = [None] * 4
    for step in range(4):
        for m in range(4):
            dx, to_y = (step + m) % 4, (y + m + 4 - z) % 4
            for dc in range(2):
                to_x, to_c = (x + dx) % 4, (c + dc) % 2
                src, dst, received = held.at[to_y, to_x * 2 + to_c], landed.at[z, mine], grad_recv.at[z, mine]
                to = device(y, to_x, to_c, to_y)
                if dx or dc:
                    send(src, dst, grad_sent.at[4], received, to)
                else:
                    alone[m] = jnp.logical_and(y == z, to_y == y)

                    @pl.when(alone[m])
                    def _():
                        pltpu.make_async_copy(src, dst, received).start()

                    @pl.when(jnp.logical_not(alone[m]))
                    def _():
                        send(src, dst, grad_sent.at[m], received, to)

    olds = (
        (attn_master, mlp_master),
        (attn_first, mlp_first),
        (attn_second, mlp_second),
        (attn_average, mlp_average),
    )

    def load(k):
        attn, mlp = olds[k]

        def fetch(cb, carry):
            for m in range(4):
                pltpu.make_async_copy(attn.at[:, cb, m, :], state_attn.at[k, cb, m], state_sem.at[0]).start()
            for m in range(3):
                pltpu.make_async_copy(mlp.at[:, cb, m, :], state_mlp.at[k, cb, m], state_sem.at[1]).start()
            return carry

        lax.fori_loop(0, 16, fetch, 0)

    load(0)
    load(1)
    load(2)
    value = sums[0]
    for k in range(len(PLANE)):
        wait_for(sums.at[2 + k], sum_recv.at[2 + k])
        value = value + sums[2 + k]
    sums[1] = value
    load(3)
    ahead = 2 + len(PLANE)
    for dy in range(1, 4):
        to = device(z, x, c, (y + dy) % 4)
        send(sums.at[1], sums.at[ahead + dy - 1], sum_sent.at[1], sum_recv.at[ahead + dy - 1], to)
    value = sums[1]
    for dy in range(3):
        wait_for(sums.at[ahead + dy], sum_recv.at[ahead + dy])
        value = value + sums[ahead + dy]
    grand = jnp.sum(value, keepdims=True)
    clip = jnp.minimum(1.0, clip_level / jnp.sqrt(grand / COUNT + 1e-06))

    wait_for(state_attn, state_sem.at[0])
    wait_for(state_mlp, state_sem.at[1])

    low = low_lanes(ROWS)

    def column(step, dz):
        return (x + 4 - (step + y + dz) % 4) % 4

    def work(step):
        def one(dz):
            source, xs = (z + dz) % 4, column(step, dz)
            for dc in range(2):
                wait_for(landed.at[source, xs * 2 + dc], grad_recv.at[source, xs * 2 + dc])
            cb = source * 4 + xs
            even, odd = split_halves(landed[source, xs * 2].astype(F32), landed[source, xs * 2 + 1].astype(F32))
            pieces = (
                (state_attn, 0, 0, 16, even[0:16]),
                (state_attn, 2, 0, 16, even[16:32]),
                (state_mlp, 0, 0, 40, even[32:72]),
                (state_mlp, 2, 0, 24, even[72:96]),
                (state_attn, 1, 0, 16, odd[0:16]),
                (state_attn, 3, 0, 16, odd[16:32]),
                (state_mlp, 1, 0, 40, odd[32:72]),
                (state_mlp, 2, 24, 16, odd[72:88]),
            )
            new = []
            for state, m, lo, n, g in pieces:
                rows = pl.ds(lo, n)
                values = advance(g, *(state[k, cb, m, rows, :] for k in range(4)), clip)
                for k in range(4):
                    state[k, cb, m, rows, :] = values[k]
                new.append(values[0])
            first_half = jnp.concatenate(new[:4], axis=0)
            other = pltpu.roll(jnp.concatenate(new[4:] + [jnp.zeros((8, 128), F32)], axis=0), 64, 1)
            held_back[dz, xs * 2] = jnp.where(low, first_half, other).astype(BF16)
            held_back[dz, xs * 2 + 1] = jnp.where(low, other, first_half).astype(BF16)

        def give(dz, may_stay):
            xs = column(step, dz)
            for dc in range(2):
                src, received = held_back.at[dz, xs * 2 + dc], back_plane_recv.at[z, mine]
                stays = jnp.logical_and(xs == x, c == dc) if may_stay else False

                def start(dst):
                    if may_stay:

                        @pl.when(stays)
                        def _():
                            pltpu.make_async_copy(src, dst, received).start()

                        @pl.when(jnp.logical_not(stays))
                        def _():
                            send(src, dst, back_plane_sent.at[0], received, device(z, xs, dc, y))

                    else:
                        send(src, dst, back_plane_sent.at[1], received, device((z + dz) % 4, xs, dc, y))

                @pl.when(y == z)
                def _():
                    start(back.at[y, mine])

                @pl.when(y != z)
                def _():
                    start(relay.at[z, mine])

        def distant(dz, carry):
            one(dz)

            @pl.when(dz > 1)
            def _():
                give(dz - 1, False)

            return carry

        lax.fori_loop(1, 4, distant, 0)
        one(0)
        give(3, False)
        return functools.partial(give, 0, True)

    def spread(step):
        def group(k, carry):
            dz = (k + y) % 4
            from_z, from_x = (z + 4 - dz) % 4, (x + step + y + dz) % 4

            @pl.when(from_z != y)
            def _():
                for dc in range(2):
                    xc = from_x * 2 + dc
                    wait_for(relay.at[from_z, xc], back_plane_recv.at[from_z, xc])
                    send(relay.at[from_z, xc], back.at[y, xc], back_ring_sent, back_ring_recv.at[y, xc], device(z, x, c, from_z))

            return carry

        lax.fori_loop(0, 4, group, 0)

    news = (
        (attn_master_new, mlp_master_new),
        (attn_first_new, mlp_first_new),
        (attn_second_new, mlp_second_new),
        (attn_average_new, mlp_average_new),
    )

    def store(step):
        def one(dz, carry):
            cb = (z + dz) % 4 * 4 + column(step, dz)
            for k, (attn, mlp) in enumerate(news):
                for m in range(4):
                    pltpu.make_async_copy(state_attn.at[k, cb, m], attn.at[:, cb, m, :], flat_sem.at[0]).start()
                for m in range(3):
                    pltpu.make_async_copy(state_mlp.at[k, cb, m], mlp.at[:, cb, m, :], flat_sem.at[1]).start()
            return carry

        lax.fori_loop(0, 4, one, 0)

    own = work(0)
    for step in range(1, 4):
        following = work(step)
        own()
        own = following
    own()
    for step in range(4):
        spread(step)
        store(step)
    for xc in range(8):
        wait_for(back.at[y, xc], back_plane_recv.at[y, xc])
        for dy in range(1, 4):
            src = (y + dy) % 4
            wait_for(back.at[src, xc], back_ring_recv.at[src, xc])

    wait_for(sums.at[pl.ds(2, len(PLANE))], sum_sent.at[0])
    wait_for(sums.at[pl.ds(2, 3)], sum_sent.at[1])
    wait_for(held_back.at[:, pl.ds(0, 7)], grad_sent.at[4])
    for m in range(4):

        @pl.when(jnp.logical_not(alone[m]))
        def _():
            wait_for(held.at[0, 0], grad_sent.at[m])

    wait_for(held_back.at[pl.ds(0, 3)], back_ring_sent)
    wait_for(held_back.at[0, pl.ds(0, 7)], back_plane_sent.at[0])
    wait_for(held_back.at[pl.ds(0, 3)], back_plane_sent.at[1])
    wait_for(state_attn, flat_sem.at[0])
    wait_for(state_mlp, flat_sem.at[1])


def run_exchange(args):
    dma = pltpu.SemaphoreType.DMA
    any_spec = pl.BlockSpec(memory_space=pl.ANY)
    return pl.pallas_call(
        exchange_kernel,
        name="exchange",
        out_shape=(
            *[jax.ShapeDtypeStruct((16, 16, 4, 128), F32)] * 4,
            *[jax.ShapeDtypeStruct((40, 16, 3, 128), F32)] * 4,
            jax.ShapeDtypeStruct((4, 8, ROWS, 128), BF16),
        ),
        in_specs=[pl.BlockSpec(memory_space=pltpu.HBM)] * 10,
        out_specs=[any_spec] * 9,
        scratch_shapes=[
            pltpu.VMEM((2, 128, 512), F32),
            pltpu.VMEM((2, 128, 1280), F32),
            pltpu.VMEM((2, 512, 128), F32),
            pltpu.VMEM((2, 1288, 128), F32),
            pltpu.VMEM((4, 8, ROWS, 128), BF16),
            pltpu.VMEM((4, 8, ROWS, 128), BF16),
            pltpu.VMEM((4, 8, ROWS, 128), BF16),
            pltpu.VMEM((4, 8, ROWS, 128), BF16),
            pltpu.VMEM((4, 16, 4, 16, 128), F32),
            pltpu.VMEM((4, 16, 3, 40, 128), F32),
            pltpu.VMEM((36, 1, 128), F32),
            dma((2,)),
            dma((2,)),
            dma((2,)),
            dma((36,)),
            dma((2,)),
            dma((4, 8)),
            dma((5,)),
            dma((4, 8)),
            dma((4, 8)),
            dma,
            dma((2,)),
        ],
        compiler_params=pltpu.CompilerParams(collective_id=0, has_side_effects=True, vmem_limit_bytes=32 << 20),
    )(*args)


def finish_kernel(*refs):
    news, back, outs = refs[:8], refs[8], refs[9:17]
    attn_weights, mlp_weights, turned_attn, turned_mlp, sem = refs[17:]
    c = lax.axis_index("shard") % 2
    for k in range(8):
        pltpu.make_async_copy(news[k], outs[k], sem.at[k]).start()
    turned_mlp[1, pl.ds(1280, 8), :] = jnp.zeros((8, 128), F32)

    def unpack(xc, carry):
        for src in range(4):
            j = xc * 4 + src
            chunk = back[src, xc].astype(F32)
            turned_attn[0, pl.ds(pl.multiple_of(j * 16, 16), 16), :] = chunk[0:16]
            turned_attn[1, pl.ds(pl.multiple_of(j * 16, 16), 16), :] = chunk[16:32]
            turned_mlp[0, pl.ds(pl.multiple_of(j * 40, 8), 40), :] = chunk[32:72]
            tail = chunk[72:96]
            turn = pltpu.roll(tail, 64, 1)
            straight = lax.broadcast(c, (24, 128)) == 0
            turned_mlp[1, pl.ds(pl.multiple_of(j * 40, 8), 24), :] = jnp.where(straight, tail, turn)
            turned_mlp[1, pl.ds(pl.multiple_of(j * 40 + 24, 8), 16), :] = jnp.where(straight, turn, tail)[:16]
        return carry

    lax.fori_loop(0, 8, unpack, 0)
    for b in range(4):
        cols = slice(b * 128, (b + 1) * 128)
        for pair in range(2):
            block = turned_attn[pair, cols, :].T.astype(BF16)
            for half in range(2):
                attn_weights[2 * pair + (half + c) % 2, :, cols] = block[64 * half : 64 * half + 64]
    for b in range(10):
        cols = slice(b * 128, (b + 1) * 128)
        block = turned_mlp[0, cols, :].T.astype(BF16)
        for half in range(2):
            mlp_weights[(half + c) % 2, :, cols] = block[64 * half : 64 * half + 64]
        mlp_weights[2, :, cols] = turned_mlp[1, cols, :].T[:64].astype(BF16)
    for k in range(8):
        pltpu.make_async_copy(news[k], outs[k], sem.at[k]).wait()


def run_finish(news, back):
    any_spec = pl.BlockSpec(memory_space=pl.ANY)
    vmem = pl.BlockSpec(memory_space=pltpu.VMEM)
    return pl.pallas_call(
        finish_kernel,
        name="finish",
        out_shape=(
            *[jax.ShapeDtypeStruct(v.shape, F32) for v in news],
            jax.ShapeDtypeStruct((4, 64, 512), BF16),
            jax.ShapeDtypeStruct((3, 64, 1280), BF16),
        ),
        in_specs=[any_spec] * 8 + [vmem],
        out_specs=[pl.BlockSpec(memory_space=pltpu.HBM)] * 8 + [vmem] * 2,
        scratch_shapes=[
            pltpu.VMEM((2, 512, 128), F32),
            pltpu.VMEM((2, 1288, 128), F32),
            pltpu.SemaphoreType.DMA((8,)),
        ],
        compiler_params=pltpu.CompilerParams(vmem_limit_bytes=24 << 20),
    )(*news, back)


def rows_first(flat, rows):
    return flat.reshape(flat.shape[0], rows, 16, 128).transpose(1, 2, 0, 3)


def members_first(value):
    rows, _, members, _ = value.shape
    return value.transpose(2, 0, 1, 3).reshape(members, rows * D)


def per_device(attn_grads, mlp_grads, *states):
    states = [rows_first(v, 16) for v in states[:4]] + [rows_first(v, 40) for v in states[4:]]
    args = [attn_grads.transpose(0, 2, 1), mlp_grads.transpose(0, 2, 1), *states]
    *news, back = run_exchange([pltpu.with_memory_space_constraint(v, pltpu.HBM) for v in args])
    *outs, attn_weights, mlp_weights = run_finish(news, back)
    outs = [members_first(v) for v in outs]
    return (*outs, attn_weights.transpose(0, 2, 1), mlp_weights.transpose(0, 2, 1))


def solution(mesh):
    whole = P(None, "tensor", "shard")
    flat = P(None, ("shard", "tensor"))
    return jax.shard_map(
        per_device,
        mesh=mesh,
        in_specs=(whole,) * 2 + (flat,) * 8,
        out_specs=(flat,) * 8 + (whole,) * 2,
        check_vma=False,
    )
```
